768 devices in a mesh: win: 192 (over y, z_lo, x), tok: 4 (over z_hi, core).
Axes of the slice: x: 4, y: 8, z: 12 (z_hi: 2, z_lo: 6; z = z_hi * 6 + z_lo), core: 2. Of those that a mesh axis runs over, the one named last changes fastest.
Arguments:
- field_tokens: bfloat16 [192, 40, 40, 1280], P('win', 'tok'), may hold values from -60 to 60
- lon_shift: int32 [4], replicated, may hold values from 1 to 20, as said below
- norm_gain: float32 [1280], replicated, may hold values from 0.1 to 1.9
- qkv_weight: bfloat16 [1280, 1920], replicated, may hold values from -1 to 1
- out_weight: bfloat16 [640, 1280], replicated, may hold values from -0.25 to 0.25
Outputs:
- result: bfloat16 [192, 40, 40, 1280], P('win', 'tok')
The draws below stay inside these ranges and needn't reach their ends.
Inputs may be any that keep to these rules, and one draw needn't show every extreme that they name: `lon_shift`: one entry is 20 and another is 1.
All inputs are finite; a program needn't handle non-finite values.
Results may differ from the reference program's by a relative error of at most 0.0046.
Values may be sent and summed in bfloat16 or wider, within the bound.
A program may use at most 64 MiB of HBM per device.

```python
import jax
import jax.numpy as jnp
from jax import lax

D = 1280
HEADS = 8
HD = 80
WS = 40
LAT_WINDOWS = 4
WINDOWS = 192
N_WIN = 192


def draw_lon_shift(key, part):
    sample = jax.random.randint(jax.random.fold_in(key, 11), (LAT_WINDOWS,), 1, WS // 2 + 1)
    chosen = jax.random.permutation(jax.random.fold_in(key, 12), LAT_WINDOWS)
    sample = sample.at[chosen[0]].set(WS // 2)
    sample = sample.at[chosen[1]].set(1)
    return sample.astype(jnp.int32)


def draw_qkv_weight(key, part):
    width = HEADS * HD
    sample = jax.random.normal(jax.random.fold_in(key, 21), (D, 3 * width), jnp.float32) * (2.0 / D) ** 0.5
    return jnp.clip(sample, -1.0, 1.0).astype(jnp.bfloat16)


def draw_field_tokens(key, part):
    shape = (WINDOWS, WS, WS, D)
    sample = jnp.clip(jax.random.normal(jax.random.fold_in(key, 31), shape, jnp.float32), -6.0, 6.0)
    return sample.astype(jnp.bfloat16)


def scatter_about(key, dims, scale, reach, kind=jnp.bfloat16):
    array = jax.random.normal(key, dims, jnp.float32) * scale
    return jnp.minimum(jnp.maximum(array, -reach), reach).astype(kind)


def setup_inputs(seed: int = 0) -> dict:
    key_of = jax.random.split(jax.random.key(seed), 6)
    return {
        "field_tokens": draw_field_tokens(jax.random.fold_in(key_of[5], 71), 0),
        "lon_shift": draw_lon_shift(jax.random.fold_in(key_of[5], 71), 0),
        "norm_gain": jnp.clip(1.0 + 0.18 * jax.random.normal(key_of[2], (D,), jnp.float32), 0.1, 1.9),
        "qkv_weight": draw_qkv_weight(jax.random.fold_in(key_of[5], 71), 0),
        "out_weight": scatter_about(key_of[4], (HEADS * HD, D), (HEADS * HD) ** -0.5, 0.25),
    }


def window_block(window, norm_gain, qkv_weight, out_weight):
    count = WS * WS
    tokens = window.reshape(count, D)
    values = tokens.astype(jnp.float32)
    factor = lax.rsqrt(lax.optimization_barrier(jnp.mean(values * values, axis=-1, keepdims=True)) + 1e-06)
    normed = (values * factor * norm_gain.astype(jnp.float32)).astype(jnp.bfloat16)
    qkv = jnp.dot(normed, qkv_weight, preferred_element_type=jnp.float32).astype(jnp.bfloat16)
    qkv = qkv.reshape(count, 3, HEADS, HD)
    queries = qkv[:, 0].astype(jnp.float32)
    key_rows = qkv[:, 1].astype(jnp.float32)
    value_rows = qkv[:, 2].astype(jnp.float32)
    scores = jnp.einsum('qhd,khd->hqk', queries, key_rows) * HD ** (-0.5)
    row_top = lax.optimization_barrier(jnp.max(scores, axis=-1, keepdims=True))
    exponent = jnp.exp(scores - row_top)
    weights = (exponent / lax.optimization_barrier(jnp.sum(exponent, axis=-1, keepdims=True))).astype(jnp.bfloat16)
    attended = jnp.einsum('hqk,khd->qhd', weights.astype(jnp.float32), value_rows).astype(jnp.bfloat16)
    projected = jnp.dot(attended.reshape(count, HEADS * HD), out_weight, preferred_element_type=jnp.float32)
    return (values + projected).astype(jnp.bfloat16).reshape(WS, WS, D)

def to_band(windows):
    lon_count = N_WIN // LAT_WINDOWS
    band = windows.reshape(lon_count, LAT_WINDOWS, WS, WS, D).transpose(1, 2, 0, 3, 4)
    return band.reshape(LAT_WINDOWS, WS, lon_count * WS, D)

def from_band(band):
    lon_count = N_WIN // LAT_WINDOWS
    windows = band.reshape(LAT_WINDOWS, WS, lon_count, WS, D).transpose(2, 0, 1, 3, 4)
    return windows.reshape(N_WIN, WS, WS, D)

def reference(field_tokens, lon_shift, norm_gain, qkv_weight, out_weight):
    band = to_band(field_tokens)
    moved = jax.vmap(lambda band_rows, amount: jnp.roll(band_rows, -amount, axis=1))(band, lon_shift)
    windows = from_band(moved)
    mixed = lax.map(lambda window: window_block(window, norm_gain, qkv_weight, out_weight), windows)
    mixed_band = to_band(mixed)
    restored = jax.vmap(lambda band_rows, amount: jnp.roll(band_rows, amount, axis=1))(mixed_band, lon_shift)
    return from_band(restored)
```

```python
import functools

import jax
import jax.numpy as jnp
from jax import lax
from jax.experimental import pallas as pl
from jax.experimental.pallas import tpu as pltpu
from jax.sharding import PartitionSpec as P

HEADS = 8
HD = 80
LAT_WINDOWS = 4
ZLO = 6
ROWS = 10
COLS = 40
D = 1280
WIDTH = HEADS * HD
EAST = 24
REST = COLS - EAST
NM = ROWS * EAST
NO = ROWS * REST
NT = NM + NO
GROUP = 4
QW = 384
QB = 160
MESH = pl.DeviceIdType.MESH
CHUNKS = ((0, 256), (256, 128), (384, 128), (512, 128))
RETURNS = ((0, 256), (256, 128))
F32 = jnp.float32
BF16 = jnp.bfloat16


def kernel(
    shift_ref, gain_ref, x_hbm, w_hbm, wo_hbm, out_ref,
    xv, xe, wv, wo, nb, kv, kvo, qa, qs, pb, lb, ao, ai, rt,
    load_sem, shift_s, shift_r, ko_s, ko_r, km_s, km_r, sib_s, sib_r, ret_s, ret_r,
):
    win, tok = lax.axis_index("win"), lax.axis_index("tok")
    n_win = 192
    core = tok % 2
    half = tok // 2
    other = 1 - core
    sib = (win, half * 2 + other)
    anti = ((win, (1 - half) * 2), (win, (1 - half) * 2 + 1))
    east_w = (win + LAT_WINDOWS) % n_win
    west_w = (win + n_win - LAT_WINDOWS) % n_win
    east, east_sib = (east_w, tok), (east_w, half * 2 + other)
    west, west_sib = (west_w, tok), (west_w, half * 2 + other)

    loads = [
        pltpu.make_async_copy(x_hbm.at[0], xv, load_sem.at[0]),
        pltpu.make_async_copy(w_hbm, wv, load_sem.at[1]),
        pltpu.make_async_copy(wo_hbm.at[pl.ds(0, 320)], wo.at[0, pl.ds(64, 320)], load_sem.at[2]),
        pltpu.make_async_copy(wo_hbm.at[pl.ds(320, 320)], wo.at[1, pl.ds(64, 320)], load_sem.at[3]),
    ]
    for c in loads:
        c.start()

    barrier = pltpu.get_barrier_semaphore()
    peers = (east, east_sib, west, west_sib, sib, anti[0], anti[1])
    for d in peers:
        pl.semaphore_signal(barrier, inc=1, device_id=d, device_id_type=MESH)
    wo[:, 0:64, :] = jnp.zeros((2, 64, D), BF16)
    pl.semaphore_wait(barrier, len(peers))

    def remote(src, dst, s, r, d):
        return pltpu.make_async_remote_copy(
            src_ref=src, dst_ref=dst, send_sem=s, recv_sem=r, device_id=d, device_id_type=MESH
        )

    shift = remote(x_hbm.at[0, :, pl.ds(0, EAST), :], xe, shift_s, shift_r, west)
    shift.start()

    offset = shift_ref[win % LAT_WINDOWS]
    gain = gain_ref[...]

    def project(values, row0, count):
        factor = lax.rsqrt(jnp.mean(values * values, axis=-1, keepdims=True) + 1e-06)
        nb[pl.ds(0, count), :] = (values * factor * gain).astype(BF16)
        normed = nb[pl.ds(0, count), :]
        rows = pl.ds(row0, count)

        def part(i):
            return jnp.dot(normed, wv[:, i * WIDTH : (i + 1) * WIDTH], preferred_element_type=F32)

        lane = lax.broadcasted_iota(jnp.int32, (count, 128), 1)
        low = lane < 64
        k = part(1)
        v = part(2)
        rk = pltpu.roll(k[:, 256:640], 320, 1)
        rv = pltpu.roll(v[:, 0:384], 64, 1)
        g0 = [k[:, 0:256], jnp.where(low, k[:, 256:384], rv[:, 0:128]), rv[:, 128:384]]
        g1 = [rk[:, 0:256], jnp.where(low, rk[:, 256:384], v[:, 256:384]), v[:, 384:640]]
        lanes = ((0, 256), (256, 384), (384, 640))
        first = core == 0
        for (a, b), u0, u1 in zip(lanes, g0, g1):
            kvo[0, rows, a:b] = u0.astype(BF16)
            kvo[1, rows, a:b] = u1.astype(BF16)
            kv[0, rows, a:b] = jnp.where(first, u0, u1).astype(BF16)
        q = part(0)
        q0 = q[:, 0:384]
        q1 = pltpu.roll(q[:, 256:640], 320, 1)
        qa[rows, :] = jnp.where(first, q0, q1).astype(BF16)
        qs[rows, :] = jnp.where(first, q1, q0).astype(BF16)

    loads[0].wait()
    own_rest = xv[:, EAST:COLS, :].astype(F32).reshape(NO, D)
    loads[1].wait()
    project(own_rest, NM, NO)
    tail, sib_tail = pl.ds(NM, NO), pl.ds(NT + NM, NO)
    head, sib_head = pl.ds(0, NM), pl.ds(NT, NM)
    sib_all = pl.ds(NT, NT)
    sends = [shift]
    ko = [
        remote(kvo.at[g, tail, :], kv.at[2 + core, tail, :], ko_s.at[g], ko_r.at[core], anti[g])
        for g in range(2)
    ]
    sib_o = [
        remote(kvo.at[other, tail, :], kv.at[1, tail, :], sib_s.at[0], sib_r.at[0], sib),
        remote(qs.at[tail, :], qa.at[sib_tail, :], sib_s.at[1], sib_r.at[1], sib),
    ]
    for c in ko + sib_o:
        c.start()
    sends += ko + sib_o

    column = lax.broadcasted_iota(jnp.int32, (ROWS, EAST, 1), 1)
    from_east = column < offset
    own_east = xv[:, 0:EAST, :].astype(F32)
    shift.wait_recv()
    mixed = jnp.where(from_east, xe[...].astype(F32), own_east).reshape(NM, D)
    project(mixed, 0, NM)
    sib_m = [
        remote(kvo.at[other, head, :], kv.at[1, head, :], sib_s.at[2], sib_r.at[2], sib),
        remote(qs.at[head, :], qa.at[sib_head, :], sib_s.at[3], sib_r.at[3], sib),
    ]
    km = []
    for i, (a, n) in enumerate(CHUNKS):
        for g in range(2):
            km.append(
                remote(
                    kvo.at[g, head, pl.ds(a, n)], kv.at[2 + core, head, pl.ds(a, n)],
                    km_s.at[i, g], km_r.at[i, core], anti[g],
                )
            )
    for c in km + sib_m:
        c.start()
    sends += km + sib_m

    for c in sib_o + sib_m:
        c.wait_recv()
    for s in range(2):
        remote(kvo.at[0, tail, :], kv.at[2 + s, tail, :], ko_s.at[0], ko_r.at[s], anti[0]).wait_recv()

    def arrived(i):
        a, n = CHUNKS[i]
        for s in range(2):
            remote(
                kvo.at[0, head, pl.ds(a, n)], kv.at[2 + s, head, pl.ds(a, n)],
                km_s.at[i, 0], km_r.at[i, s], anti[0],
            ).wait_recv()

    scale = HD ** (-0.5) * 1.4426950408889634

    def scores(h):
        a = (80 * h) // 128 * 128
        b = (80 * h + 79) // 128 * 128 + 128
        lane = lax.broadcasted_iota(jnp.int32, (QB, b - a), 1) + a
        keep = (lane >= 80 * h) & (lane < 80 * h + 80)
        keys = kv.at[:, :, pl.ds(a, b - a)]

        @pl.loop(0, 2 * NT // QB)
        def _(i):
            rows = pl.ds(pl.multiple_of(i * QB, QB), QB)
            q = jnp.where(keep, qa[rows, a:b].astype(F32), 0.0).astype(BF16)
            s = lax.dot_general(
                q, keys[...].reshape(4 * NT, b - a), (((1,), (1,)), ((), ())), preferred_element_type=F32
            )
            top = jnp.max(s, axis=-1, keepdims=True)
            e = jnp.exp2((s - top) * scale)
            lb[h, rows, :] = 1.0 / jnp.sum(e, axis=-1, keepdims=True)
            pb[h, rows, :] = e.astype(BF16)

    def values(lanes, heads):
        a, n = lanes
        lane = lax.broadcasted_iota(jnp.int32, (QB, n), 1) + a

        @pl.loop(0, 2 * NT // QB)
        def _(i):
            rows = pl.ds(pl.multiple_of(i * QB, QB), QB)
            total = jnp.zeros((QB, n), F32)
            vals = kv[:, :, 256 + a : 256 + a + n].reshape(4 * NT, n)
            for h in heads:
                o = jnp.dot(pb[h, rows, :], vals, preferred_element_type=F32) * lb[h, rows, :]
                first = 64 + 80 * h
                total = jnp.where((lane >= first) & (lane < first + 80), o, total)
            ao[rows, a : a + n] = total.astype(BF16)

    arrived(0)
    scores(0)
    scores(1)
    scores(2)
    arrived(1)
    scores(3)
    arrived(2)
    back = []

    def give(i):
        a, n = RETURNS[i]
        l = pl.ds(a, n)
        cs = [
            remote(ao.at[head, l], rt.at[core, :, l], ret_s.at[i, 0], ret_r.at[i, core], east),
            remote(ao.at[sib_head, l], rt.at[core, :, l], ret_s.at[i, 1], ret_r.at[i, core], east_sib),
            remote(ao.at[sib_all, l], ai.at[:, l], ret_s.at[i, 2], ret_r.at[i, 2], sib),
        ]
        for c in cs:
            c.start()
        return cs

    values((0, 256), (0, 1, 2))
    sends += give(0)
    arrived(3)
    values((256, 128), (2, 3))
    sends += give(1)

    loads[2].wait()
    loads[3].wait()

    for i, (a, n) in enumerate(RETURNS):
        l = pl.ds(a, n)
        remote(ao.at[sib_all, l], ai.at[:, l], ret_s.at[i, 2], ret_r.at[i, 2], sib).wait_recv()
    rest = jnp.dot(ao[NM:NT, :], wo[core], preferred_element_type=F32)
    rest += jnp.dot(ai[NM:NT, :], wo[other], preferred_element_type=F32)
    own_rest = xv[:, EAST:COLS, :].astype(F32)
    out_ref[0, :, EAST:COLS, :] = (own_rest + rest.reshape(ROWS, REST, D)).astype(BF16)

    for i, (a, n) in enumerate(RETURNS):
        l = pl.ds(a, n)
        for s in range(2):
            remote(ao.at[head, l], rt.at[s, :, l], ret_s.at[i, 0], ret_r.at[i, s], east).wait_recv()
    away = from_east

    def pick(far, near):
        far3 = far.astype(F32).reshape(ROWS, EAST, QW)
        near3 = near.astype(F32).reshape(ROWS, EAST, QW)
        return jnp.where(away, far3, near3).reshape(NM, QW).astype(BF16)

    moved = jnp.dot(pick(rt[core], ao[0:NM, :]), wo[core], preferred_element_type=F32)
    moved += jnp.dot(pick(rt[other], ai[0:NM, :]), wo[other], preferred_element_type=F32)
    own_east = xv[:, 0:EAST, :].astype(F32)
    out_ref[0, :, 0:EAST, :] = (own_east + moved.reshape(ROWS, EAST, D)).astype(BF16)

    for c in sends:
        c.wait_send()


def shards(field_tokens, lon_shift, norm_gain, qkv_weight, out_weight):
    any_spec = pl.BlockSpec(memory_space=pl.ANY)
    dma = pltpu.SemaphoreType.DMA
    return pl.pallas_call(
        kernel,
        out_shape=jax.ShapeDtypeStruct((1, ROWS, COLS, D), BF16),
        in_specs=[
            pl.BlockSpec(memory_space=pltpu.SMEM),
            pl.BlockSpec(memory_space=pltpu.VMEM),
            any_spec, any_spec, any_spec,
        ],
        out_specs=pl.BlockSpec(memory_space=pltpu.VMEM),
        scratch_shapes=[
            pltpu.VMEM((ROWS, COLS, D), BF16),
            pltpu.VMEM((ROWS, EAST, D), BF16),
            pltpu.VMEM((D, 3 * WIDTH), BF16),
            pltpu.VMEM((2, QW, D), BF16),
            pltpu.VMEM((NM, D), BF16),
            pltpu.VMEM((4, NT, WIDTH), BF16),
            pltpu.VMEM((2, NT, WIDTH), BF16),
            pltpu.VMEM((2 * NT, QW), BF16),
            pltpu.VMEM((NT, QW), BF16),
            pltpu.VMEM((GROUP, 2 * NT, 4 * NT), BF16),
            pltpu.VMEM((GROUP, 2 * NT, 1), F32),
            pltpu.VMEM((2 * NT, QW), BF16),
            pltpu.VMEM((NT, QW), BF16),
            pltpu.VMEM((2, NM, QW), BF16),
            dma((4,)),
            dma(()), dma(()),
            dma((2,)), dma((2,)),
            dma((4, 2)), dma((4, 2)),
            dma((4,)), dma((4,)),
            dma((2, 3)), dma((2, 3)),
        ],
        name="window_attention",
        compiler_params=pltpu.CompilerParams(collective_id=0, has_side_effects=True),
    )(lon_shift, norm_gain.reshape(1, D), field_tokens, qkv_weight, out_weight)


def solution(mesh):
    placed = (P("win", "tok", None, None), P(), P(), P(), P())
    return jax.shard_map(
        shards, mesh=mesh, in_specs=placed, out_specs=P("win", "tok", None, None), check_vma=False
    )
```
